32 devices in a mesh: mem: 2 (over y), sx: 4 (over z), sy: 4 (over x, core).
Axes of the slice: x: 2, y: 2, z: 4, core: 2. Of those that a mesh axis runs over, the one named last changes fastest.
Arguments:
- child: bfloat16 [8, 8, 192, 3072], P('mem', None, 'sx', 'sy'), may hold values from -13 to 13
Outputs:
- parent_mean: float32 [8, 64, 1024], P('mem', 'sx', 'sy')
- local_cov: float32 [64, 64, 1024], P('mem', 'sx', 'sy')
The draws below stay inside these ranges and needn't reach their ends.
All inputs are finite; a program needn't handle non-finite values.
Results may differ from the reference program's by a relative error of at most 0.002.
Values sent between devices are 32-bit elements; how exact they have to be, the bound alone decides.
No kernel may reach another device: no remote copies, remote signals or barrier semaphores. Data moves between devices by JAX's collectives and lax.ppermute only.
A program may use at most 192 MiB of HBM per device.

```python
import jax
import jax.numpy as jnp
import numpy as np
from jax import lax

L = 8
HALO = 4
M = 8
NX = 64
NY = 1024


def draw_child(key, part):
    base_key = jax.random.fold_in(key, 11)
    noise_key = jax.random.fold_in(key, 12)
    rows = 3 * NX
    cols = 3 * NY
    xpos = jnp.arange(rows, dtype=jnp.float32) / max(rows - 1, 1)
    xscale = (1.0 + 2.0 * xpos)[None, None, :, None]
    base = jax.random.uniform(base_key, (1, L, rows, cols), jnp.float32, -1.0, 1.0)
    noise = jax.random.truncated_normal(noise_key, -4.0, 4.0, (M, L, rows, cols), jnp.float32)
    values = base + xscale * noise
    return values.astype(jnp.bfloat16)


def setup_inputs(seed: int = 0) -> dict:
    splits = jax.random.split(jax.random.key(seed), 2)
    return {
        "child": draw_child(jax.random.fold_in(splits[1], 71), 0),
    }


def gaspari_table(reach):
    offsets = np.arange(-reach, reach + 1) * 1.0
    dist = np.sqrt(offsets[:, None] ** 2 + offsets[None, :] ** 2) / 2.5
    near = -0.25 * dist ** 5 + 0.5 * dist ** 4 + 0.625 * dist ** 3 - 5.0 / 3.0 * dist ** 2 + 1.0
    safe = np.maximum(dist, 0.001)
    far = dist ** 5 / 12.0 - 0.5 * dist ** 4 + 0.625 * dist ** 3 + 5.0 / 3.0 * dist ** 2 - 5.0 * dist + 4.0 - 2.0 / (3.0 * safe)
    table = np.where(dist <= 1.0, near, np.where(dist < 2.0, far, 0.0))
    return table / table.sum()

def reference(child):
    parent = lax.optimization_barrier(jnp.sum(child.reshape(M, L, NX, 3, NY, 3), axis=(3, 5), dtype=jnp.float32)) / 9.0
    parent_mean = lax.optimization_barrier(jnp.sum(parent, axis=0)) / M
    anomaly = parent - parent_mean[None]
    cov = jnp.einsum('alxy,akxy->lkxy', anomaly, anomaly) / (M - 1)
    cov = cov.reshape(L * L, NX, NY)
    diag = jnp.stack([cov[l * L + l] for l in range(L)])
    spread = jnp.sum(diag) / (L * NX * NY)
    table = gaspari_table(HALO)
    padded = jnp.pad(cov, ((0, 0), (HALO, HALO), (HALO, HALO)))
    smoothed = jnp.zeros((L * L, NX, NY), jnp.float32)
    for a in range(2 * HALO + 1):
        for b in range(2 * HALO + 1):
            weight = float(table[a, b])
            if weight != 0.0:
                smoothed = smoothed + weight * padded[:, a:a + NX, b:b + NY]
    return (parent_mean, smoothed / (spread + 1e-06))
```

```python
import functools
import math

import jax
import jax.numpy as jnp
import numpy as np
from jax import lax
from jax.experimental import pallas as pl
from jax.experimental.pallas import tpu as pltpu
from jax.sharding import PartitionSpec as P

REACH = 4
FACTOR = 3
SUB = 8
LANES = 128
SIDES = 2 * REACH
VMEM = pl.BlockSpec(memory_space=pltpu.VMEM)
SMEM = pl.BlockSpec(memory_space=pltpu.SMEM)
HBM = pl.BlockSpec(memory_space=pl.ANY)
F32 = jnp.float32
BF16 = jnp.bfloat16


def gaspari_table(reach):
    offsets = np.arange(-reach, reach + 1) * 1.0
    dist = np.sqrt(offsets[:, None] ** 2 + offsets[None, :] ** 2) / 2.5
    near = -0.25 * dist**5 + 0.5 * dist**4 + 0.625 * dist**3 - 5.0 / 3.0 * dist**2 + 1.0
    safe = np.maximum(dist, 0.001)
    far = (
        dist**5 / 12.0
        - 0.5 * dist**4
        + 0.625 * dist**3
        + 5.0 / 3.0 * dist**2
        - 5.0 * dist
        + 4.0
        - 2.0 / (3.0 * safe)
    )
    table = np.where(dist <= 1.0, near, np.where(dist < 2.0, far, 0.0))
    return table / table.sum()


def window_matrices(cols):
    table = gaspari_table(REACH)

    def weight(di, dj):
        inside = (abs(di) <= REACH) & (abs(dj) <= REACH)
        return np.where(inside, table[np.clip(di, -REACH, REACH) + REACH, np.clip(dj, -REACH, REACH) + REACH], 0.0)

    src, dst = np.arange(cols)[:, None], np.arange(cols)[None, :]
    main = np.concatenate([weight(np.full((cols, cols), d), src - dst) for d in range(REACH + 1)])
    columns = np.concatenate([np.arange(-REACH, 0), np.arange(cols, cols + REACH)])
    side = np.zeros((LANES, REACH * cols))
    for block in range(3):
        for row in range(REACH):
            for col in range(SIDES):
                lane = (block * REACH + row) * SIDES + col
                for to in range(REACH):
                    di = block * REACH + row - to - REACH
                    side[lane, to * cols : (to + 1) * cols] = weight(
                        np.full((cols,), di), columns[col] - np.arange(cols)
                    )
    return main, side


def split_constant(x):
    high = x.astype(BF16)
    return high, (x - high.astype(np.float64)).astype(BF16)


def lanes(start, width):
    lane = lax.broadcasted_iota(jnp.int32, (SUB, LANES), 1)
    return (lane >= start) & (lane < start + width)


def pool_kernel(members, child, s_ref, h_ref, right_ref, left_ref, buf, pmat, t_ref, q_ref, sem):
    md, levels, child_rows, child_cols = child.shape
    rows, cols = child_rows // FACTOR, child_cols // FACTOR
    halves = cols // LANES
    copies = [pltpu.make_async_copy(child.at[m], buf.at[m], sem.at[m]) for m in range(md)]
    for copy in copies:
        copy.start()
    k = lax.broadcasted_iota(jnp.int32, (child_cols, cols), 0)
    n = lax.broadcasted_iota(jnp.int32, (child_cols, cols), 1)
    gap = k - FACTOR * n
    pmat[...] = jnp.where((gap >= 0) & (gap < FACTOR), 1.0, 0.0).astype(BF16)
    for m in range(md):
        copies[m].wait()
        x = buf[m].reshape(levels * child_rows, child_cols)
        y = jnp.dot(x, pmat[...], preferred_element_type=F32)
        for h in range(halves):
            t_ref[m, h] = y[:, h * LANES : (h + 1) * LANES]
        for i in range(rows):
            for h in range(halves):
                parts = [
                    t_ref[m, h, pl.ds(FACTOR * i + a, levels, stride=child_rows), :]
                    for a in range(FACTOR)
                ]
                q_ref[m, i * halves + h] = parts[0] + parts[1] + parts[2]
    norm = 1.0 / (FACTOR * FACTOR * math.sqrt(members - 1))
    partial = jnp.zeros((SUB, LANES), F32)
    for g in range(rows // REACH):
        right = jnp.zeros((SUB, LANES), F32)
        left = jnp.zeros((SUB, LANES), F32)
        for ri in range(REACH):
            i = g * REACH + ri
            for h in range(halves):
                slot = i * halves + h
                fields = []
                total = q_ref[0, slot]
                for c in range(1, md):
                    p = q_ref[c, slot]
                    contrast = (total - c * p) * (norm / math.sqrt(c * (c + 1)))
                    fields.append(contrast)
                    partial = partial + contrast * contrast
                    h_ref[(i * (md - 1) + c - 1) * halves + h] = contrast
                    total = total + p
                s_ref[slot] = total
                fields = [total] + fields
                for c, v in enumerate(fields):
                    base = (c * REACH + ri) * SIDES
                    if h == halves - 1:
                        moved = pltpu.roll(v, (base - (LANES - REACH)) % LANES, 1)
                        right = jnp.where(lanes(base, REACH), moved, right)
                    if h == 0:
                        moved = pltpu.roll(v, (base + REACH) % LANES, 1)
                        left = jnp.where(lanes(base + REACH, REACH), moved, left)
        right_ref[g] = right
        left_ref[g] = left
    s_ref[rows * halves] = partial


def pool(child, members):
    md, levels, child_rows, child_cols = child.shape
    rows, cols = child_rows // FACTOR, child_cols // FACTOR
    halves = cols // LANES
    tile = (SUB, LANES)
    return pl.pallas_call(
        functools.partial(pool_kernel, members),
        out_shape=(
            jax.ShapeDtypeStruct((rows * halves + 1,) + tile, F32),
            jax.ShapeDtypeStruct((rows * (md - 1) * halves,) + tile, F32),
            jax.ShapeDtypeStruct((rows // REACH,) + tile, F32),
            jax.ShapeDtypeStruct((rows // REACH,) + tile, F32),
        ),
        in_specs=[HBM],
        out_specs=(VMEM,) * 4,
        scratch_shapes=[
            pltpu.VMEM(child.shape, BF16),
            pltpu.VMEM((child_cols, cols), BF16),
            pltpu.VMEM((md, halves, levels * child_rows, LANES), F32),
            pltpu.VMEM((md, rows * halves) + tile, F32),
            pltpu.SemaphoreType.DMA((md,)),
        ],
        name="pool",
    )(child)


def group_contrasts(sums, md, members):
    norm = 1.0 / (FACTOR * FACTOR * math.sqrt((members - 1) * md))
    total, out = sums[0], []
    for g in range(1, len(sums)):
        out.append((total - g * sums[g]) * (norm / math.sqrt(g * (g + 1))))
        total = total + sums[g]
    return out, total


def mean_kernel(groups, md, level_dev, first_ref, *refs):
    s_refs = refs[:groups]
    mean_ref, partial_ref, m_ref = refs[groups:]
    rows, cols = mean_ref.shape[1:]
    halves = cols // LANES
    members = groups * md
    partial = functools.reduce(jnp.add, [s[rows * halves] for s in s_refs])
    scale = 1.0 / (FACTOR * FACTOR * members)
    for i in range(rows):
        for h in range(halves):
            contrasts, total = group_contrasts([s[i * halves + h] for s in s_refs], md, members)
            for v in contrasts:
                partial = partial + v * v
            m_ref[h, pl.ds(i, SUB, stride=rows), :] = total * scale
    for l in range(level_dev):
        start = pl.multiple_of((first_ref[0] + l) * rows, SUB)
        for h in range(halves):
            mean_ref[l, :, h * LANES : (h + 1) * LANES] = m_ref[h, pl.ds(start, rows), :]
    partial_ref[...] = partial


def mean(first, sums, md, level_dev, rows, cols):
    return pl.pallas_call(
        functools.partial(mean_kernel, len(sums), md, level_dev),
        out_shape=(
            jax.ShapeDtypeStruct((level_dev, rows, cols), F32),
            jax.ShapeDtypeStruct((SUB, LANES), F32),
        ),
        in_specs=[SMEM] + [VMEM] * len(sums),
        out_specs=(VMEM, VMEM),
        scratch_shapes=[pltpu.VMEM((cols // LANES, SUB * rows, LANES), F32)],
        name="mean",
    )(first, *sums)


def cov_kernel(groups, md, level_dev, rows, halves, first_ref, *refs):
    s_refs, h_refs, e_refs = refs[:groups], refs[groups : 2 * groups], refs[2 * groups : 3 * groups]
    top_ref, mid_ref, bottom_ref, d_ref, x_ref = refs[3 * groups :]
    members = groups * md
    first = first_ref[0]
    edge = REACH * level_dev * halves

    def target(i):
        if i < REACH:
            return top_ref, i
        if i < rows - REACH:
            return mid_ref, i - REACH
        return bottom_ref, i - (rows - REACH)

    def spread_row(ref, slot, l):
        return jnp.broadcast_to(ref[slot, pl.ds(first + l, 1), :], (SUB, LANES))

    for i in range(rows):
        out, row = target(i)
        for h in range(halves):
            slot = i * halves + h
            contrasts, _ = group_contrasts([s[slot] for s in s_refs], md, members)
            where = []
            for g, v in enumerate(contrasts):
                d_ref[g * rows * halves + slot] = v
                where.append((d_ref, g * rows * halves + slot))
            for ref in h_refs:
                where += [(ref, (i * (md - 1) + c) * halves + h) for c in range(md - 1)]
            values = [ref[at] for ref, at in where]
            for l in range(level_dev):
                acc = None
                for (ref, at), v in zip(where, values):
                    term = spread_row(ref, at, l) * v
                    acc = term if acc is None else acc + term
                out[(row * level_dev + l) * halves + h] = acc

    width = LANES // md
    for b in range(rows // REACH):
        packs = [e[b] for e in e_refs]
        contrasts, _ = group_contrasts(packs, md, members)
        for g in range(groups):
            inner = jnp.zeros((SUB, LANES), F32) if g == 0 else contrasts[g - 1]
            x_ref[b * groups + g] = jnp.where(lanes(0, width), inner, packs[g])
        pack = jnp.zeros((SUB, LANES), F32)
        for l in range(level_dev):
            acc = None
            for g in range(groups):
                term = spread_row(x_ref, b * groups + g, l) * x_ref[b * groups + g]
                acc = term if acc is None else acc + term
            total = acc
            for c in range(1, md):
                total = total + pltpu.roll(acc, c * width, 1)
            pack = jnp.where(lanes(l * width, width), total, pack)
        out, row = target(b * REACH)
        base = out.shape[0] - (out.shape[0] // (edge + 1))
        out[base + row // REACH] = pack


def cov(first, sums, contrasts, packs, md, level_dev, rows, halves):
    groups = len(sums)
    edge = REACH * level_dev * halves + 1
    blocks = rows // REACH - 2
    tile = (SUB, LANES)
    return pl.pallas_call(
        functools.partial(cov_kernel, groups, md, level_dev, rows, halves),
        out_shape=(
            jax.ShapeDtypeStruct((edge,) + tile, F32),
            jax.ShapeDtypeStruct((edge * blocks,) + tile, F32),
            jax.ShapeDtypeStruct((edge,) + tile, F32),
        ),
        in_specs=[SMEM] + [VMEM] * (3 * groups),
        out_specs=(VMEM,) * 3,
        scratch_shapes=[
            pltpu.VMEM(((groups - 1) * rows * halves,) + tile, F32),
            pltpu.VMEM((groups * (rows // REACH),) + tile, F32),
        ],
        name="cov",
    )(first, *sums, *contrasts, *packs)


def smooth_kernel(cells, level_dev, above, top, mid, bottom, below, part, wm, wml, ws, wsl, out, x_hi, x_lo, e_hi, e_lo, o_ref):
    _, rows, cols = out.shape
    halves = cols // LANES
    edge = REACH * level_dev * halves
    refs = [above, top] + [mid] * (rows // REACH - 2) + [bottom, below]

    def cell(e, l, h):
        block, row = divmod(e, REACH)
        ref = refs[block]
        if ref is mid:
            row += (block - 2) * REACH
        return ref[(row * level_dev + l) * halves + h]

    def pack(block):
        ref = refs[block]
        if ref is mid:
            return ref[edge * (rows // REACH - 2) + block - 2]
        return ref[edge]

    def put(high, low, at, columns, v):
        hi = v.astype(BF16)
        high[at : at + 2 * SUB, columns] = hi
        low[at : at + 2 * SUB, columns] = (v - hi.astype(F32)).astype(BF16)

    order = [(i, l) for i in range(rows) for l in range(level_dev)]
    for q in range(0, len(order), 2):
        for h in range(halves):
            for d in range(REACH + 1):
                pair = []
                for i, l in order[q : q + 2]:
                    v = cell(i + REACH - d, l, h)
                    if d:
                        v = v + cell(i + REACH + d, l, h)
                    pair.append(v)
                columns = slice(d * cols + h * LANES, d * cols + (h + 1) * LANES)
                put(x_hi, x_lo, q * SUB, columns, jnp.concatenate(pair, axis=0))
    width = REACH * SIDES
    order = [(b, l) for b in range(rows // REACH) for l in range(level_dev)]
    for q in range(0, len(order), 2):
        pair = []
        for b, l in order[q : q + 2]:
            v = jnp.zeros((SUB, LANES), F32)
            for g in range(3):
                moved = pack(b + g)
                if g != l:
                    moved = pltpu.roll(moved, ((g - l) * width) % LANES, 1)
                v = jnp.where(lanes(g * width, width), moved, v)
            pair.append(v)
        put(e_hi, e_lo, q * SUB, slice(0, LANES), jnp.concatenate(pair, axis=0))

    def product(high, low, w, wl):
        y = jnp.dot(high[...], w[...], preferred_element_type=F32)
        y = y + jnp.dot(low[...], w[...], preferred_element_type=F32)
        return y + jnp.dot(high[...], wl[...], preferred_element_type=F32)

    y = product(x_hi, x_lo, wm, wml)
    z = product(e_hi, e_lo, ws, wsl)
    spread = jnp.sum(part[...], keepdims=True) / cells
    inverse = 1.0 / (spread + 1e-06)
    for i in range(rows):
        b, ri = divmod(i, REACH)
        for l in range(level_dev):
            for h in range(halves):
                v = y[(i * level_dev + l) * SUB : (i * level_dev + l + 1) * SUB, h * LANES : (h + 1) * LANES]
                at = (b * level_dev + l) * SUB
                v = v + z[at : at + SUB, ri * cols + h * LANES : ri * cols + (h + 1) * LANES]
                o_ref[h, pl.ds(l * SUB * rows + i, SUB, stride=rows), :] = v * inverse
    for h in range(halves):
        out[:, :, h * LANES : (h + 1) * LANES] = o_ref[h].reshape(level_dev * SUB, rows, LANES)


def smooth(above, top, mid, bottom, below, part, cells, level_dev, rows, cols):
    main, side = window_matrices(cols)
    wm, wml = split_constant(main)
    ws, wsl = split_constant(side)
    edge_rows = rows // REACH * level_dev * SUB
    return pl.pallas_call(
        functools.partial(smooth_kernel, cells, level_dev),
        out_shape=jax.ShapeDtypeStruct((level_dev * SUB, rows, cols), F32),
        in_specs=[VMEM] * 10,
        out_specs=VMEM,
        scratch_shapes=[
            pltpu.VMEM((rows * level_dev * SUB, (REACH + 1) * cols), BF16),
            pltpu.VMEM((rows * level_dev * SUB, (REACH + 1) * cols), BF16),
            pltpu.VMEM((edge_rows, LANES), BF16),
            pltpu.VMEM((edge_rows, LANES), BF16),
            pltpu.VMEM((cols // LANES, level_dev * SUB * rows, LANES), F32),
        ],
        name="smooth",
    )(above, top, mid, bottom, below, part, wm, wml, ws, wsl)


def shift(x, axis, by):
    devices = lax.axis_size(axis)
    return lax.ppermute(x, axis, [(i, i + by) for i in range(devices) if 0 <= i + by < devices])


def rotate(x, axis, by):
    devices = lax.axis_size(axis)
    return lax.ppermute(x, axis, [(i, (i + by) % devices) for i in range(devices)])


def everyone(x, axis):
    return [x] + [rotate(x, axis, by) for by in range(1, lax.axis_size(axis))]


def local(child):
    md, levels, child_rows, child_cols = child.shape
    rows, cols = child_rows // FACTOR, child_cols // FACTOR
    halves = cols // LANES
    groups = lax.axis_size("mem")
    members = md * groups
    level_dev = levels // groups
    first = (lax.axis_index("mem") * level_dev).astype(jnp.int32).reshape(1)
    s, h, right, left = pool(child, members)
    sums = everyone(s, "mem")
    contrasts = everyone(h, "mem")
    from_left, from_right = shift(right, "sy", 1), shift(left, "sy", -1)
    lane = lax.broadcasted_iota(jnp.int32, from_left.shape, 2)
    pack = jnp.where(lane % SIDES < REACH, from_left, from_right)
    packs = everyone(pack, "mem")
    parent_mean, part = mean(first, sums, md, level_dev, rows, cols)
    for axis in ("sx", "sy"):
        part = functools.reduce(jnp.add, everyone(part, axis))
    top, mid, bottom = cov(first, sums, contrasts, packs, md, level_dev, rows, halves)
    above, below = shift(bottom, "sx", 1), shift(top, "sx", -1)
    cells = levels * rows * lax.axis_size("sx") * cols * lax.axis_size("sy")
    local_cov = smooth(above, top, mid, bottom, below, part, cells, level_dev, rows, cols)
    return (parent_mean, local_cov)


def solution(mesh):
    in_specs = (P("mem", None, "sx", "sy"),)
    out_specs = (P("mem", "sx", "sy"), P("mem", "sx", "sy"))
    return jax.shard_map(local, mesh=mesh, in_specs=in_specs, out_specs=out_specs, check_vma=False)
```

```python
import functools
import math

import jax
import jax.numpy as jnp
import numpy as np
from jax import lax
from jax.experimental import pallas as pl
from jax.experimental.pallas import tpu as pltpu
from jax.sharding import PartitionSpec as P


PAIRED = ("sx", "sy")
STEPS = (('sx', 0), ('sx', 1), ('sy', 1), ('sy', 0))

REACH = 4
FACTOR = 3
SUB = 8
LANES = 128
SIDES = 2 * REACH
VMEM = pl.BlockSpec(memory_space=pltpu.VMEM)
SMEM = pl.BlockSpec(memory_space=pltpu.SMEM)
HBM = pl.BlockSpec(memory_space=pltpu.HBM)
LIMIT = pltpu.CompilerParams(vmem_limit_bytes=16 << 20)
F32 = jnp.float32
BF16 = jnp.bfloat16


def gaspari_table(reach):
    offsets = np.arange(-reach, reach + 1) * 1.0
    dist = np.sqrt(offsets[:, None] ** 2 + offsets[None, :] ** 2) / 2.5
    near = -0.25 * dist**5 + 0.5 * dist**4 + 0.625 * dist**3 - 5.0 / 3.0 * dist**2 + 1.0
    safe = np.maximum(dist, 0.001)
    far = (
        dist**5 / 12.0
        - 0.5 * dist**4
        + 0.625 * dist**3
        + 5.0 / 3.0 * dist**2
        - 5.0 * dist
        + 4.0
        - 2.0 / (3.0 * safe)
    )
    table = np.where(dist <= 1.0, near, np.where(dist < 2.0, far, 0.0))
    return table / table.sum()


def window_matrices(cols):
    table = gaspari_table(REACH)

    def weight(di, dj):
        inside = (abs(di) <= REACH) & (abs(dj) <= REACH)
        return np.where(inside, table[np.clip(di, -REACH, REACH) + REACH, np.clip(dj, -REACH, REACH) + REACH], 0.0)

    src, dst = np.arange(cols)[:, None], np.arange(cols)[None, :]
    main = np.concatenate([weight(np.full((cols, cols), d), src - dst) for d in range(REACH + 1)])
    columns = np.concatenate([np.arange(-REACH, 0), np.arange(cols, cols + REACH)])
    side = np.zeros((LANES, REACH * cols))
    for block in range(3):
        for row in range(REACH):
            for col in range(SIDES):
                lane = (block * REACH + row) * SIDES + col
                for to in range(REACH):
                    di = block * REACH + row - to - REACH
                    side[lane, to * cols : (to + 1) * cols] = weight(
                        np.full((cols,), di), columns[col] - np.arange(cols)
                    )
    return main, side


def rounded_window():
    table = gaspari_table(REACH)
    best = None
    for factor in np.linspace(1.0, 2.0, 4097)[:-1]:
        error = (table * factor).astype(BF16).astype(np.float64) / factor - table
        worst = max(np.sqrt((error**2).sum() / (table**2).sum()), abs(error.sum()))
        if best is None or worst < best[0]:
            best = (worst, factor)
    return best[1]


def lanes(start, width):
    lane = lax.broadcasted_iota(jnp.int32, (SUB, LANES), 1)
    return (lane >= start) & (lane < start + width)


def placed(i, rows):
    if i < REACH:
        return True, i
    if i < rows - REACH:
        return False, i - REACH
    return True, i - (rows - SIDES)


def pool_kernel(members, child, s_ref, edge_ref, mid_ref, right_ref, left_ref, buf, pmat, even_ref, odd_ref, sem):
    md, levels, child_rows, child_cols = child.shape
    rows, cols = child_rows // FACTOR, child_cols // FACTOR
    halves = cols // LANES
    wide = FACTOR * LANES
    copies = [pltpu.make_async_copy(child.at[m], buf.at[m], sem.at[m]) for m in range(md)]
    for copy in copies:
        copy.start()
    gap = lax.broadcasted_iota(jnp.int32, (wide, LANES), 0) - FACTOR * lax.broadcasted_iota(
        jnp.int32, (wide, LANES), 1
    )
    pmat[...] = jnp.where((gap >= 0) & (gap < FACTOR), 1.0, 0.0).astype(BF16)
    place = lax.broadcasted_iota(jnp.int32, (SUB, LANES), 1) >> (REACH.bit_length() - 1)
    norm = 1.0 / (FACTOR * FACTOR * math.sqrt(members - 1))
    partial = jnp.zeros((SUB, LANES), F32)

    def packed(g, c, sides):
        for ref, values, spare in ((right_ref, sides[0], LANES - REACH), (left_ref, sides[1], -REACH)):
            pack = ref[g]
            for ri, v in enumerate(values):
                base = (c * REACH + ri) * SIDES
                at = base // REACH + (spare < 0)
                pack = jnp.where(place == at, pltpu.roll(v, (base - spare) % LANES, 1), pack)
            ref[g] = pack

    for g in range(rows // REACH):
        right_ref[g] = jnp.zeros((SUB, LANES), F32)
        left_ref[g] = jnp.zeros((SUB, LANES), F32)
    blocks = rows // REACH

    sums_of = (even_ref, odd_ref)
    height = levels * child_rows
    chunk = levels // 2
    products = halves * (levels // chunk)

    def product(m, n):
        h, start = n % halves, n // halves * chunk
        x = buf[m, start : start + chunk, :, h * wide : (h + 1) * wide].reshape(chunk * child_rows, wide)
        at = h * height + start * child_rows
        sums_of[m % 2][at : at + chunk * child_rows, :] = jnp.dot(x, pmat[...], preferred_element_type=F32)

    def fields(m, g, partial):
        contrasts, totals = ([], []), ([], [])
        for ri in range(REACH):
            i = g * REACH + ri
            outer, at = placed(i, rows)
            h_ref = edge_ref if outer else mid_ref
            for h in range(halves):
                slot = i * halves + h
                parts = [
                    sums_of[m % 2][pl.ds(h * height + FACTOR * i + a, levels, stride=child_rows), :]
                    for a in range(FACTOR)
                ]
                p = parts[0] + parts[1] + parts[2]
                if m == 0:
                    s_ref[slot] = p
                    continue
                total = s_ref[slot]
                contrast = (total - m * p) * (norm / math.sqrt(m * (m + 1)))
                total = total + p
                h_ref[(at * (md - 1) + m - 1) * halves + h] = contrast
                s_ref[slot] = total
                partial = partial + contrast * contrast
                if h == halves - 1:
                    contrasts[0].append(contrast)
                    totals[0].append(total)
                if h == 0:
                    contrasts[1].append(contrast)
                    totals[1].append(total)
        if m > 0:
            packed(g, m, contrasts)
        if m == md - 1:
            packed(g, 0, totals)
        return partial

    for m in range(md + 1):
        if m < md:
            copies[m].wait()
        for n in range(max(products, blocks)):
            if m < md and n < products:
                product(m, n)
            if m > 0 and n < blocks:
                partial = fields(m - 1, n, partial)
    s_ref[rows * halves] = partial


def pool(child, members):
    md, levels, child_rows, child_cols = child.shape
    rows, cols = child_rows // FACTOR, child_cols // FACTOR
    halves = cols // LANES
    tile = (SUB, LANES)
    return pl.pallas_call(
        functools.partial(pool_kernel, members),
        out_shape=(
            jax.ShapeDtypeStruct((rows * halves + 1,) + tile, F32),
            jax.ShapeDtypeStruct((SIDES * (md - 1) * halves,) + tile, F32),
            jax.ShapeDtypeStruct(((rows - SIDES) * (md - 1) * halves,) + tile, F32),
            jax.ShapeDtypeStruct((rows // REACH,) + tile, F32),
            jax.ShapeDtypeStruct((rows // REACH,) + tile, F32),
        ),
        in_specs=[HBM],
        out_specs=(VMEM,) * 5,
        scratch_shapes=[
            pltpu.VMEM(child.shape, BF16),
            pltpu.VMEM((FACTOR * LANES, LANES), BF16),
            pltpu.VMEM((halves * levels * child_rows, LANES), F32),
            pltpu.VMEM((halves * levels * child_rows, LANES), F32),
            pltpu.SemaphoreType.DMA((md,)),
        ],
        compiler_params=LIMIT,
        name="pool",
    )(pltpu.with_memory_space_constraint(child, pltpu.HBM))


def group_contrasts(sums, md, members):
    norm = 1.0 / (FACTOR * FACTOR * math.sqrt((members - 1) * md))
    total, out = sums[0], []
    for g in range(1, len(sums)):
        out.append((total - g * sums[g]) * (norm / math.sqrt(g * (g + 1))))
        total = total + sums[g]
    return out, total


def partial_kernel(groups, md, *refs):
    s_refs, partial_ref = refs[:groups], refs[groups]
    slots = s_refs[0].shape[0] - 1
    partial = functools.reduce(jnp.add, [s[slots] for s in s_refs])
    for slot in range(slots):
        contrasts, _ = group_contrasts([s[slot] for s in s_refs], md, groups * md)
        for v in contrasts:
            partial = partial + v * v
    partial_ref[...] = partial


def partial_variance(sums, md):
    return pl.pallas_call(
        functools.partial(partial_kernel, len(sums), md),
        out_shape=jax.ShapeDtypeStruct((SUB, LANES), F32),
        in_specs=[VMEM] * len(sums),
        out_specs=VMEM,
        compiler_params=LIMIT,
        name="partial",
    )(*sums)


def spread_row(ref, slot, row):
    return jnp.broadcast_to(ref[slot, pl.ds(row, 1), :], (SUB, LANES))


def cov_rows(chosen, first, level_dev, rows, halves, md, s_refs, h_refs, d_ref, store):
    groups = len(s_refs)
    for n, i in enumerate(chosen):
        _, at = placed(i, rows)
        for h in range(halves):
            contrasts, _ = group_contrasts([s[i * halves + h] for s in s_refs], md, groups * md)
            where = []
            for g, v in enumerate(contrasts):
                slot = (n * halves + h) * (groups - 1) + g
                d_ref[slot] = v
                where.append((d_ref, slot))
            for ref in h_refs:
                where += [(ref, (at * (md - 1) + c) * halves + h) for c in range(md - 1)]
            values = [ref[slot] for ref, slot in where]
            for l in range(level_dev):
                acc = None
                for (ref, slot), v in zip(where, values):
                    term = spread_row(ref, slot, first + l) * v
                    acc = term if acc is None else acc + term
                store(i, l, h, acc)


def cov_packs(chosen, first, level_dev, md, e_refs, x_ref, store):
    groups = len(e_refs)
    width = LANES // md
    for n, b in enumerate(chosen):
        packs = [e[b] for e in e_refs]
        contrasts, _ = group_contrasts(packs, md, groups * md)
        for g in range(groups):
            inner = jnp.zeros((SUB, LANES), F32) if g == 0 else contrasts[g - 1]
            x_ref[n * groups + g] = jnp.where(lanes(0, width), inner, packs[g])
        pack = jnp.zeros((SUB, LANES), F32)
        for l in range(level_dev):
            acc = None
            for g in range(groups):
                term = spread_row(x_ref, n * groups + g, first + l) * x_ref[n * groups + g]
                acc = term if acc is None else acc + term
            total = acc
            for c in range(1, md):
                total = total + pltpu.roll(acc, c * width, 1)
            pack = jnp.where(lanes(l * width, width), total, pack)
        store(b, pack)


def smooth_rows(chosen, cell, pack, level_dev, cols, x_ref, e_ref, weights):
    halves = cols // LANES

    def put(ref, at, columns, v):
        hi = v.astype(BF16)
        ref[at : at + 2 * SUB, columns] = hi
        at += ref.shape[0] // 2
        ref[at : at + 2 * SUB, columns] = (v - hi.astype(F32)).astype(BF16)

    order = [(i, l) for i in chosen for l in range(level_dev)]
    for q in range(0, len(order), 2):
        for h in range(halves):
            for d in range(REACH + 1):
                pair = []
                for i, l in order[q : q + 2]:
                    v = cell(i - d, l, h)
                    if d:
                        v = v + cell(i + d, l, h)
                    pair.append(v)
                columns = slice(d * cols + h * LANES, d * cols + (h + 1) * LANES)
                put(x_ref, q * SUB, columns, jnp.concatenate(pair, axis=0))
    width = REACH * SIDES
    blocks = sorted({i // REACH for i in chosen})
    order = [(b, l) for b in blocks for l in range(level_dev)]
    for q in range(0, len(order), 2):
        pair = []
        for b, l in order[q : q + 2]:
            v = jnp.zeros((SUB, LANES), F32)
            for g in range(3):
                moved = pack(b + g - 1)
                if g != l:
                    moved = pltpu.roll(moved, ((g - l) * width) % LANES, 1)
                v = jnp.where(lanes(g * width, width), moved, v)
            pair.append(v)
        put(e_ref, q * SUB, slice(0, LANES), jnp.concatenate(pair, axis=0))

    def product(ref, w):
        both = jnp.dot(ref[...], w[...], preferred_element_type=F32)
        return both[: ref.shape[0] // 2] + both[ref.shape[0] // 2 :]

    y = product(x_ref, weights[0])
    z = product(e_ref, weights[1])

    def value(i, l, h):
        n = chosen.index(i)
        at = (blocks.index(i // REACH) * level_dev + l) * SUB
        side = (i % REACH) * cols + h * LANES
        return (
            y[(n * level_dev + l) * SUB : (n * level_dev + l + 1) * SUB, h * LANES : (h + 1) * LANES]
            + z[at : at + SUB, side : side + LANES]
        )

    return value


def scratch_of(chosen, level_dev, cols):
    rows = len(chosen) * level_dev * SUB
    sides = rows // REACH
    return [
        pltpu.VMEM((2 * rows, (REACH + 1) * cols), BF16),
        pltpu.VMEM((2 * sides, LANES), BF16),
    ]


def outer_rows(rows):
    return list(range(REACH)) + list(range(rows - REACH, rows))


def inner_rows(rows):
    return list(range(REACH, rows - REACH))


def edge_kernel(groups, md, level_dev, rows, halves, first_ref, *refs):
    s_refs, h_refs, e_refs = refs[:groups], refs[groups : 2 * groups], refs[2 * groups : 3 * groups]
    top_ref, bottom_ref, d_ref, x_ref = refs[3 * groups :]
    first = first_ref[0]
    edge = REACH * level_dev * halves

    def store(i, l, h, v):
        ref = top_ref if i < REACH else bottom_ref
        ref[(i % REACH * level_dev + l) * halves + h] = v

    def store_pack(b, v):
        ref = top_ref if b == 0 else bottom_ref
        ref[edge] = v

    cov_packs([0, rows // REACH - 1], first, level_dev, md, e_refs, x_ref, store_pack)
    cov_rows(outer_rows(rows), first, level_dev, rows, halves, md, s_refs, h_refs, d_ref, store)


def edge_cov(first, sums, contrasts, packs, md, level_dev, rows, halves):
    groups = len(sums)
    shape = jax.ShapeDtypeStruct((REACH * level_dev * halves + 1, SUB, LANES), F32)
    return pl.pallas_call(
        functools.partial(edge_kernel, groups, md, level_dev, rows, halves),
        out_shape=(shape, shape),
        in_specs=[SMEM] + [VMEM] * (3 * groups),
        out_specs=(VMEM, VMEM),
        scratch_shapes=[
            pltpu.VMEM(((groups - 1) * SIDES * halves, SUB, LANES), F32),
            pltpu.VMEM((groups * 2, SUB, LANES), F32),
        ],
        compiler_params=LIMIT,
        name="edge",
    )(first, *sums, *contrasts, *packs)


def inner_kernel(groups, md, level_dev, rows, cols, first_ref, *refs):
    s_refs, h_refs, e_refs = refs[:groups], refs[groups : 2 * groups], refs[2 * groups : 3 * groups]
    top, bottom, wm, ws, mid_ref, o_ref, d_ref, x_ref = refs[3 * groups : 3 * groups + 8]
    scratch = refs[3 * groups + 8 :]
    halves = cols // LANES
    first = first_ref[0]
    edge = REACH * level_dev * halves
    base = (rows - SIDES) * level_dev * halves

    def store(i, l, h, v):
        mid_ref[((i - REACH) * level_dev + l) * halves + h] = v

    def store_pack(b, v):
        mid_ref[base + b - 1] = v

    inner = inner_rows(rows)
    last = rows // REACH - 1
    cov_packs(list(range(1, last)), first, level_dev, md, e_refs, x_ref, store_pack)
    cov_rows(inner, first, level_dev, rows, halves, md, s_refs, h_refs, d_ref, store)

    def cell(i, l, h):
        if i < REACH:
            return top[(i * level_dev + l) * halves + h]
        if i >= rows - REACH:
            return bottom[((i - rows + REACH) * level_dev + l) * halves + h]
        return mid_ref[((i - REACH) * level_dev + l) * halves + h]

    def pack(b):
        if b == 0:
            return top[edge]
        return bottom[edge] if b == last else mid_ref[base + b - 1]

    value = smooth_rows(inner, cell, pack, level_dev, cols, *scratch, (wm, ws))
    for i in inner:
        for l in range(level_dev):
            for h in range(halves):
                o_ref[h, pl.ds(l * SUB * rows + i, SUB, stride=rows), :] = value(i, l, h)


def inner_smooth(first, sums, contrasts, packs, top, bottom, weights, md, level_dev, rows, cols):
    groups = len(sums)
    halves = cols // LANES
    slots = (rows - SIDES) * level_dev * halves + rows // REACH - 2
    inner = inner_rows(rows)
    return pl.pallas_call(
        functools.partial(inner_kernel, groups, md, level_dev, rows, cols),
        out_shape=(
            jax.ShapeDtypeStruct((slots, SUB, LANES), F32),
            jax.ShapeDtypeStruct((halves, level_dev * SUB * rows, LANES), F32),
        ),
        in_specs=[SMEM] + [VMEM] * (3 * groups + 4),
        out_specs=(VMEM, VMEM),
        scratch_shapes=[
            pltpu.VMEM(((groups - 1) * len(inner) * halves, SUB, LANES), F32),
            pltpu.VMEM((groups * (rows // REACH - 2), SUB, LANES), F32),
        ]
        + scratch_of(inner, level_dev, cols),
        compiler_params=LIMIT,
        name="inner",
    )(first, *sums, *contrasts, *packs, top, bottom, *weights)


def outer_kernel(groups, md, level_dev, rows, cols, first_ref, *refs):
    s_refs = refs[:groups]
    above, top, mid, bottom, below, wm, ws = refs[groups : groups + 7]
    mean_ref, o_ref, m_ref = refs[groups + 7 : groups + 10]
    scratch = refs[groups + 10 :]
    halves = cols // LANES
    edge = REACH * level_dev * halves
    base = (rows - SIDES) * level_dev * halves
    last = rows // REACH - 1
    first = first_ref[0]

    scale = 1.0 / (FACTOR * FACTOR * groups * md)
    for i in range(rows):
        for h in range(halves):
            total = functools.reduce(jnp.add, [s[i * halves + h] for s in s_refs])
            m_ref[h, pl.ds(i, SUB, stride=rows), :] = total * scale
    for l in range(level_dev):
        start = pl.multiple_of((first + l) * rows, SUB)
        for h in range(halves):
            mean_ref[l, :, h * LANES : (h + 1) * LANES] = m_ref[h, pl.ds(start, rows), :]

    def cell(i, l, h):
        if i < 0:
            ref, row = above, i + REACH
        elif i < REACH:
            ref, row = top, i
        elif i < rows - REACH:
            ref, row = mid, i - REACH
        elif i < rows:
            ref, row = bottom, i - rows + REACH
        else:
            ref, row = below, i - rows
        return ref[(row * level_dev + l) * halves + h]

    def pack(b):
        if 0 < b < last:
            return mid[base + b - 1]
        ref = above if b < 0 else top if b == 0 else bottom if b == last else below
        return ref[edge]

    outer = outer_rows(rows)
    value = smooth_rows(outer, cell, pack, level_dev, cols, *scratch, (wm, ws))
    for i in outer:
        for l in range(level_dev):
            for h in range(halves):
                o_ref[h, pl.ds(l * SUB * rows + i, SUB, stride=rows), :] = value(i, l, h)


def outer_smooth(first, sums, above, top, mid, bottom, below, weights, md, level_dev, rows, cols):
    groups = len(sums)
    halves = cols // LANES
    return pl.pallas_call(
        functools.partial(outer_kernel, groups, md, level_dev, rows, cols),
        out_shape=(
            jax.ShapeDtypeStruct((level_dev, rows, cols), F32),
            jax.ShapeDtypeStruct((halves, level_dev * SUB * rows, LANES), F32),
        ),
        in_specs=[SMEM] + [VMEM] * (groups + 7),
        out_specs=(VMEM, VMEM),
        scratch_shapes=[pltpu.VMEM((halves, SUB * rows, LANES), F32)]
        + scratch_of(outer_rows(rows), level_dev, cols),
        compiler_params=LIMIT,
        name="outer",
    )(first, *sums, above, top, mid, bottom, below, *weights)


def scale_kernel(cells, factor, inside, outside, part, out):
    shape = (out.shape[0], out.shape[1], LANES)
    rows = out.shape[1]
    spread = jnp.sum(part[...], keepdims=True) / cells
    inverse = (1.0 / ((spread + 1e-06) * factor))[None]
    row = lax.broadcasted_iota(jnp.int32, shape, 1)
    inner = (row >= REACH) & (row < rows - REACH)
    for h in range(out.shape[2] // LANES):
        v = jnp.where(inner, inside[h].reshape(shape), outside[h].reshape(shape))
        out[:, :, h * LANES : (h + 1) * LANES] = v * inverse


def scaled(inside, outside, part, cells, factor, pairs, rows, cols):
    return pl.pallas_call(
        functools.partial(scale_kernel, cells, float(factor)),
        out_shape=jax.ShapeDtypeStruct((pairs, rows, cols), F32),
        in_specs=[VMEM] * 3,
        out_specs=VMEM,
        compiler_params=LIMIT,
        name="scale",
    )(inside, outside, part)


def shift(x, axis, by):
    devices = lax.axis_size(axis)
    return lax.ppermute(x, axis, [(i, i + by) for i in range(devices) if 0 <= i + by < devices])


def neighbours(initial, last, axis):
    devices = lax.axis_size(axis)
    if axis not in PAIRED:
        before = shift(last, axis, 1)
        after = shift(initial, axis, -1)
        return before, after
    odd = lax.axis_index(axis) % 2 == 1
    received = []
    for parity in range(2):
        pairs = [(i, i + 1) for i in range(parity, devices - 1, 2)]
        send = jnp.where(odd, initial, last) if parity == 0 else jnp.where(odd, last, initial)
        perm = pairs + [(b, a) for a, b in pairs]
        received.append(lax.ppermute(send, axis, perm))
    return jnp.where(odd, received[0], received[1]), jnp.where(odd, received[1], received[0])


def rotate(x, axis, by):
    devices = lax.axis_size(axis)
    return lax.ppermute(x, axis, [(i, (i + by) % devices) for i in range(devices)])


def everyone(x, axis):
    return [x] + [rotate(x, axis, by) for by in range(1, lax.axis_size(axis))]


def across(x, order):
    for axis in sorted({axis for axis, _ in order}):
        devices = lax.axis_size(axis)
        if devices & (devices - 1):
            x = functools.reduce(jnp.add, everyone(x, axis))
    steps = [(axis, bit) for bit in range(32) for axis in ("sx", "sy") if 1 << bit < lax.axis_size(axis)]
    for axis, bit in sorted(steps, key=lambda step: order.index(step) if step in order else len(order)):
        devices = lax.axis_size(axis)
        if devices & (devices - 1) == 0:
            x = x + lax.ppermute(x, axis, [(i, i ^ (1 << bit)) for i in range(devices)])
    return x


def local(child):
    md, levels, child_rows, child_cols = child.shape
    rows, cols = child_rows // FACTOR, child_cols // FACTOR
    halves = cols // LANES
    groups = lax.axis_size("mem")
    level_dev = levels // groups
    first = (lax.axis_index("mem") * level_dev).astype(jnp.int32).reshape(1)
    main, side = window_matrices(cols)
    factor = rounded_window()
    weights = ((main * factor).astype(BF16), (side * factor).astype(BF16))
    s, h_edge, h_mid, right, left = pool(child, md * groups)
    sums = everyone(s, "mem")
    edges = everyone(h_edge, "mem")
    from_left, from_right = neighbours(left, right, "sy")
    lane = lax.broadcasted_iota(jnp.int32, from_left.shape, 2)
    pack = jnp.where(lane % SIDES < REACH, from_left, from_right)
    packs = everyone(pack, "mem")
    mids = everyone(h_mid, "mem")
    part = partial_variance(sums, md)
    part = across(part, STEPS)
    top, bottom = edge_cov(first, sums, edges, packs, md, level_dev, rows, halves)
    above, below = neighbours(top, bottom, "sx")
    mid, inside = inner_smooth(first, sums, mids, packs, top, bottom, weights, md, level_dev, rows, cols)
    cells = levels * rows * lax.axis_size("sx") * cols * lax.axis_size("sy")
    parent_mean, outside = outer_smooth(first, sums, above, top, mid, bottom, below, weights, md, level_dev, rows, cols)
    local_cov = scaled(inside, outside, part, cells, factor, level_dev * levels, rows, cols)
    return (parent_mean, local_cov)


def solution(mesh):
    in_specs = (P("mem", None, "sx", "sy"),)
    out_specs = (P("mem", "sx", "sy"), P("mem", "sx", "sy"))
    return jax.shard_map(local, mesh=mesh, in_specs=in_specs, out_specs=out_specs, check_vma=False)
```

```python
import functools
import math

import jax
import jax.numpy as jnp
import numpy as np
from jax import lax
from jax.experimental import pallas as pl
from jax.experimental.pallas import tpu as pltpu
from jax.sharding import PartitionSpec as P


PAIRED = ("sx", "sy")
STEPS = (('sx', 0), ('sx', 1), ('sy', 0), ('sy', 1))

REACH = 4
FACTOR = 3
SUB = 8
LANES = 128
SIDES = 2 * REACH
VMEM = pl.BlockSpec(memory_space=pltpu.VMEM)
SMEM = pl.BlockSpec(memory_space=pltpu.SMEM)
HBM = pl.BlockSpec(memory_space=pltpu.HBM)
LIMIT = pltpu.CompilerParams(vmem_limit_bytes=16 << 20)
F32 = jnp.float32
BF16 = jnp.bfloat16


def gaspari_table(reach):
    offsets = np.arange(-reach, reach + 1) * 1.0
    dist = np.sqrt(offsets[:, None] ** 2 + offsets[None, :] ** 2) / 2.5
    near = -0.25 * dist**5 + 0.5 * dist**4 + 0.625 * dist**3 - 5.0 / 3.0 * dist**2 + 1.0
    safe = np.maximum(dist, 0.001)
    far = (
        dist**5 / 12.0
        - 0.5 * dist**4
        + 0.625 * dist**3
        + 5.0 / 3.0 * dist**2
        - 5.0 * dist
        + 4.0
        - 2.0 / (3.0 * safe)
    )
    table = np.where(dist <= 1.0, near, np.where(dist < 2.0, far, 0.0))
    return table / table.sum()


def window_matrices(cols):
    table = gaspari_table(REACH)

    def weight(di, dj):
        inside = (abs(di) <= REACH) & (abs(dj) <= REACH)
        return np.where(inside, table[np.clip(di, -REACH, REACH) + REACH, np.clip(dj, -REACH, REACH) + REACH], 0.0)

    src, dst = np.arange(cols)[:, None], np.arange(cols)[None, :]
    main = np.concatenate([weight(np.full((cols, cols), d), src - dst) for d in range(REACH + 1)])
    columns = np.concatenate([np.arange(-REACH, 0), np.arange(cols, cols + REACH)])
    side = np.zeros((LANES, REACH * cols))
    for block in range(3):
        for row in range(REACH):
            for col in range(SIDES):
                lane = (block * REACH + row) * SIDES + col
                for to in range(REACH):
                    di = block * REACH + row - to - REACH
                    side[lane, to * cols : (to + 1) * cols] = weight(
                        np.full((cols,), di), columns[col] - np.arange(cols)
                    )
    return main, side


def rounded_window():
    table = gaspari_table(REACH)
    best = None
    for factor in np.linspace(1.0, 2.0, 4097)[:-1]:
        error = (table * factor).astype(BF16).astype(np.float64) / factor - table
        worst = max(np.sqrt((error**2).sum() / (table**2).sum()), abs(error.sum()))
        if best is None or worst < best[0]:
            best = (worst, factor)
    return best[1]


def lanes(start, width):
    lane = lax.broadcasted_iota(jnp.int32, (SUB, LANES), 1)
    return (lane >= start) & (lane < start + width)


def placed(i, rows):
    if i < REACH:
        return True, i
    if i < rows - REACH:
        return False, i - REACH
    return True, i - (rows - SIDES)


def pool_kernel(members, child, s_ref, edge_ref, mid_ref, right_ref, left_ref, buf, pmat, even_ref, odd_ref, sem):
    md, levels, child_rows, child_cols = child.shape
    rows, cols = child_rows // FACTOR, child_cols // FACTOR
    halves = cols // LANES
    wide = FACTOR * LANES
    copies = [pltpu.make_async_copy(child.at[m], buf.at[m], sem.at[m]) for m in range(md)]
    for copy in copies:
        copy.start()
    gap = lax.broadcasted_iota(jnp.int32, (wide, LANES), 0) - FACTOR * lax.broadcasted_iota(
        jnp.int32, (wide, LANES), 1
    )
    pmat[...] = jnp.where((gap >= 0) & (gap < FACTOR), 1.0, 0.0).astype(BF16)
    place = lax.broadcasted_iota(jnp.int32, (SUB, LANES), 1) >> (REACH.bit_length() - 1)
    norm = 1.0 / (FACTOR * FACTOR * math.sqrt(members - 1))
    partial = jnp.zeros((SUB, LANES), F32)

    def packed(g, c, sides):
        for ref, values, spare in ((right_ref, sides[0], LANES - REACH), (left_ref, sides[1], -REACH)):
            pack = ref[g]
            for ri, v in enumerate(values):
                base = (c * REACH + ri) * SIDES
                at = base // REACH + (spare < 0)
                pack = jnp.where(place == at, pltpu.roll(v, (base - spare) % LANES, 1), pack)
            ref[g] = pack

    for g in range(rows // REACH):
        right_ref[g] = jnp.zeros((SUB, LANES), F32)
        left_ref[g] = jnp.zeros((SUB, LANES), F32)
    blocks = rows // REACH

    sums_of = (even_ref, odd_ref)
    height = levels * child_rows
    chunk = levels // 2
    products = halves * (levels // chunk)

    def product(m, n):
        h, start = n % halves, n // halves * chunk
        x = buf[m, start : start + chunk, :, h * wide : (h + 1) * wide].reshape(chunk * child_rows, wide)
        at = h * height + start * child_rows
        sums_of[m % 2][at : at + chunk * child_rows, :] = jnp.dot(x, pmat[...], preferred_element_type=F32)

    def fields(m, g, partial):
        contrasts, totals = ([], []), ([], [])
        for ri in range(REACH):
            i = g * REACH + ri
            outer, at = placed(i, rows)
            h_ref = edge_ref if outer else mid_ref
            for h in range(halves):
                slot = i * halves + h
                parts = [
                    sums_of[m % 2][pl.ds(h * height + FACTOR * i + a, levels, stride=child_rows), :]
                    for a in range(FACTOR)
                ]
                p = parts[0] + parts[1] + parts[2]
                if m == 0:
                    s_ref[slot] = p
                    continue
                total = s_ref[slot]
                contrast = (total - m * p) * (norm / math.sqrt(m * (m + 1)))
                total = total + p
                h_ref[(at * (md - 1) + m - 1) * halves + h] = contrast
                s_ref[slot] = total
                partial = partial + contrast * contrast
                if h == halves - 1:
                    contrasts[0].append(contrast)
                    totals[0].append(total)
                if h == 0:
                    contrasts[1].append(contrast)
                    totals[1].append(total)
        if m > 0:
            packed(g, m, contrasts)
        if m == md - 1:
            packed(g, 0, totals)
        return partial

    for m in range(md + 1):
        if m < md:
            copies[m].wait()
        for n in range(max(products, blocks)):
            if m < md and n < products:
                product(m, n)
            if m > 0 and n < blocks:
                partial = fields(m - 1, n, partial)
    s_ref[rows * halves] = partial


def pool(child, members):
    md, levels, child_rows, child_cols = child.shape
    rows, cols = child_rows // FACTOR, child_cols // FACTOR
    halves = cols // LANES
    tile = (SUB, LANES)
    return pl.pallas_call(
        functools.partial(pool_kernel, members),
        out_shape=(
            jax.ShapeDtypeStruct((rows * halves + 1,) + tile, F32),
            jax.ShapeDtypeStruct((SIDES * (md - 1) * halves,) + tile, F32),
            jax.ShapeDtypeStruct(((rows - SIDES) * (md - 1) * halves,) + tile, F32),
            jax.ShapeDtypeStruct((rows // REACH,) + tile, F32),
            jax.ShapeDtypeStruct((rows // REACH,) + tile, F32),
        ),
        in_specs=[HBM],
        out_specs=(VMEM,) * 5,
        scratch_shapes=[
            pltpu.VMEM(child.shape, BF16),
            pltpu.VMEM((FACTOR * LANES, LANES), BF16),
            pltpu.VMEM((halves * levels * child_rows, LANES), F32),
            pltpu.VMEM((halves * levels * child_rows, LANES), F32),
            pltpu.SemaphoreType.DMA((md,)),
        ],
        compiler_params=LIMIT,
        name="pool",
    )(pltpu.with_memory_space_constraint(child, pltpu.HBM))


def group_contrasts(sums, md, members):
    norm = 1.0 / (FACTOR * FACTOR * math.sqrt((members - 1) * md))
    total, out = sums[0], []
    for g in range(1, len(sums)):
        out.append((total - g * sums[g]) * (norm / math.sqrt(g * (g + 1))))
        total = total + sums[g]
    return out, total


def partial_kernel(groups, md, *refs):
    s_refs, partial_ref = refs[:groups], refs[groups]
    slots = s_refs[0].shape[0] - 1
    partial = functools.reduce(jnp.add, [s[slots] for s in s_refs])
    for slot in range(slots):
        contrasts, _ = group_contrasts([s[slot] for s in s_refs], md, groups * md)
        for v in contrasts:
            partial = partial + v * v
    partial_ref[...] = partial


def partial_variance(sums, md):
    return pl.pallas_call(
        functools.partial(partial_kernel, len(sums), md),
        out_shape=jax.ShapeDtypeStruct((SUB, LANES), F32),
        in_specs=[VMEM] * len(sums),
        out_specs=VMEM,
        compiler_params=LIMIT,
        name="partial",
    )(*sums)


def spread_row(ref, slot, row):
    return jnp.broadcast_to(ref[slot, pl.ds(row, 1), :], (SUB, LANES))


def cov_rows(chosen, first, level_dev, rows, halves, md, s_refs, h_refs, d_ref, store):
    groups = len(s_refs)
    for n, i in enumerate(chosen):
        _, at = placed(i, rows)
        for h in range(halves):
            contrasts, _ = group_contrasts([s[i * halves + h] for s in s_refs], md, groups * md)
            where = []
            for g, v in enumerate(contrasts):
                slot = (n * halves + h) * (groups - 1) + g
                d_ref[slot] = v
                where.append((d_ref, slot))
            for ref in h_refs:
                where += [(ref, (at * (md - 1) + c) * halves + h) for c in range(md - 1)]
            values = [ref[slot] for ref, slot in where]
            for l in range(level_dev):
                acc = None
                for (ref, slot), v in zip(where, values):
                    term = spread_row(ref, slot, first + l) * v
                    acc = term if acc is None else acc + term
                store(i, l, h, acc)


def cov_packs(chosen, first, level_dev, md, e_refs, x_ref, store):
    groups = len(e_refs)
    width = LANES // md
    for n, b in enumerate(chosen):
        packs = [e[b] for e in e_refs]
        contrasts, _ = group_contrasts(packs, md, groups * md)
        for g in range(groups):
            inner = jnp.zeros((SUB, LANES), F32) if g == 0 else contrasts[g - 1]
            x_ref[n * groups + g] = jnp.where(lanes(0, width), inner, packs[g])
        pack = jnp.zeros((SUB, LANES), F32)
        for l in range(level_dev):
            acc = None
            for g in range(groups):
                term = spread_row(x_ref, n * groups + g, first + l) * x_ref[n * groups + g]
                acc = term if acc is None else acc + term
            total = acc
            for c in range(1, md):
                total = total + pltpu.roll(acc, c * width, 1)
            pack = jnp.where(lanes(l * width, width), total, pack)
        store(b, pack)


def smooth_rows(chosen, cell, pack, level_dev, cols, x_ref, e_ref, weights):
    halves = cols // LANES

    def put(ref, at, columns, v):
        hi = v.astype(BF16)
        ref[at : at + 2 * SUB, columns] = hi
        at += ref.shape[0] // 2
        ref[at : at + 2 * SUB, columns] = (v - hi.astype(F32)).astype(BF16)

    order = [(i, l) for i in chosen for l in range(level_dev)]
    for q in range(0, len(order), 2):
        for h in range(halves):
            for d in range(REACH + 1):
                pair = []
                for i, l in order[q : q + 2]:
                    v = cell(i - d, l, h)
                    if d:
                        v = v + cell(i + d, l, h)
                    pair.append(v)
                columns = slice(d * cols + h * LANES, d * cols + (h + 1) * LANES)
                put(x_ref, q * SUB, columns, jnp.concatenate(pair, axis=0))
    width = REACH * SIDES
    blocks = sorted({i // REACH for i in chosen})
    order = [(b, l) for b in blocks for l in range(level_dev)]
    for q in range(0, len(order), 2):
        pair = []
        for b, l in order[q : q + 2]:
            v = jnp.zeros((SUB, LANES), F32)
            for g in range(3):
                moved = pack(b + g - 1)
                if g != l:
                    moved = pltpu.roll(moved, ((g - l) * width) % LANES, 1)
                v = jnp.where(lanes(g * width, width), moved, v)
            pair.append(v)
        put(e_ref, q * SUB, slice(0, LANES), jnp.concatenate(pair, axis=0))

    def product(ref, w):
        both = jnp.dot(ref[...], w[...], preferred_element_type=F32)
        return both[: ref.shape[0] // 2] + both[ref.shape[0] // 2 :]

    y = product(x_ref, weights[0])
    z = product(e_ref, weights[1])

    def value(i, l, h):
        n = chosen.index(i)
        at = (blocks.index(i // REACH) * level_dev + l) * SUB
        side = (i % REACH) * cols + h * LANES
        return (
            y[(n * level_dev + l) * SUB : (n * level_dev + l + 1) * SUB, h * LANES : (h + 1) * LANES]
            + z[at : at + SUB, side : side + LANES]
        )

    return value


def scratch_of(chosen, level_dev, cols):
    rows = len(chosen) * level_dev * SUB
    sides = rows // REACH
    return [
        pltpu.VMEM((2 * rows, (REACH + 1) * cols), BF16),
        pltpu.VMEM((2 * sides, LANES), BF16),
    ]


def outer_rows(rows):
    return list(range(REACH)) + list(range(rows - REACH, rows))


def inner_rows(rows):
    return list(range(REACH, rows - REACH))


def edge_kernel(groups, md, level_dev, rows, halves, first_ref, *refs):
    s_refs, h_refs, e_refs = refs[:groups], refs[groups : 2 * groups], refs[2 * groups : 3 * groups]
    top_ref, bottom_ref, d_ref, x_ref = refs[3 * groups :]
    first = first_ref[0]
    edge = REACH * level_dev * halves

    def store(i, l, h, v):
        ref = top_ref if i < REACH else bottom_ref
        ref[(i % REACH * level_dev + l) * halves + h] = v

    def store_pack(b, v):
        ref = top_ref if b == 0 else bottom_ref
        ref[edge] = v

    cov_packs([0, rows // REACH - 1], first, level_dev, md, e_refs, x_ref, store_pack)
    cov_rows(outer_rows(rows), first, level_dev, rows, halves, md, s_refs, h_refs, d_ref, store)


def edge_cov(first, sums, contrasts, packs, md, level_dev, rows, halves):
    groups = len(sums)
    shape = jax.ShapeDtypeStruct((REACH * level_dev * halves + 1, SUB, LANES), F32)
    return pl.pallas_call(
        functools.partial(edge_kernel, groups, md, level_dev, rows, halves),
        out_shape=(shape, shape),
        in_specs=[SMEM] + [VMEM] * (3 * groups),
        out_specs=(VMEM, VMEM),
        scratch_shapes=[
            pltpu.VMEM(((groups - 1) * SIDES * halves, SUB, LANES), F32),
            pltpu.VMEM((groups * 2, SUB, LANES), F32),
        ],
        compiler_params=LIMIT,
        name="edge",
    )(first, *sums, *contrasts, *packs)


def inner_kernel(groups, md, level_dev, rows, cols, first_ref, *refs):
    s_refs, h_refs, e_refs = refs[:groups], refs[groups : 2 * groups], refs[2 * groups : 3 * groups]
    top, bottom, wm, ws, mid_ref, o_ref, d_ref, x_ref = refs[3 * groups : 3 * groups + 8]
    scratch = refs[3 * groups + 8 :]
    halves = cols // LANES
    first = first_ref[0]
    edge = REACH * level_dev * halves
    base = (rows - SIDES) * level_dev * halves

    def store(i, l, h, v):
        mid_ref[((i - REACH) * level_dev + l) * halves + h] = v

    def store_pack(b, v):
        mid_ref[base + b - 1] = v

    inner = inner_rows(rows)
    last = rows // REACH - 1
    cov_packs(list(range(1, last)), first, level_dev, md, e_refs, x_ref, store_pack)
    cov_rows(inner, first, level_dev, rows, halves, md, s_refs, h_refs, d_ref, store)

    def cell(i, l, h):
        if i < REACH:
            return top[(i * level_dev + l) * halves + h]
        if i >= rows - REACH:
            return bottom[((i - rows + REACH) * level_dev + l) * halves + h]
        return mid_ref[((i - REACH) * level_dev + l) * halves + h]

    def pack(b):
        if b == 0:
            return top[edge]
        return bottom[edge] if b == last else mid_ref[base + b - 1]

    value = smooth_rows(inner, cell, pack, level_dev, cols, *scratch, (wm, ws))
    for i in inner:
        for l in range(level_dev):
            for h in range(halves):
                o_ref[h, pl.ds(l * SUB * rows + i, SUB, stride=rows), :] = value(i, l, h)


def inner_smooth(first, sums, contrasts, packs, top, bottom, weights, md, level_dev, rows, cols):
    groups = len(sums)
    halves = cols // LANES
    slots = (rows - SIDES) * level_dev * halves + rows // REACH - 2
    inner = inner_rows(rows)
    return pl.pallas_call(
        functools.partial(inner_kernel, groups, md, level_dev, rows, cols),
        out_shape=(
            jax.ShapeDtypeStruct((slots, SUB, LANES), F32),
            jax.ShapeDtypeStruct((halves, level_dev * SUB * rows, LANES), F32),
        ),
        in_specs=[SMEM] + [VMEM] * (3 * groups + 4),
        out_specs=(VMEM, VMEM),
        scratch_shapes=[
            pltpu.VMEM(((groups - 1) * len(inner) * halves, SUB, LANES), F32),
            pltpu.VMEM((groups * (rows // REACH - 2), SUB, LANES), F32),
        ]
        + scratch_of(inner, level_dev, cols),
        compiler_params=LIMIT,
        name="inner",
    )(first, *sums, *contrasts, *packs, top, bottom, *weights)


def outer_kernel(level_dev, rows, cols, above, top, mid, bottom, below, wm, ws, o_ref, *scratch):
    halves = cols // LANES
    edge = REACH * level_dev * halves
    base = (rows - SIDES) * level_dev * halves
    last = rows // REACH - 1

    def cell(i, l, h):
        if i < 0:
            ref, row = above, i + REACH
        elif i < REACH:
            ref, row = top, i
        elif i < rows - REACH:
            ref, row = mid, i - REACH
        elif i < rows:
            ref, row = bottom, i - rows + REACH
        else:
            ref, row = below, i - rows
        return ref[(row * level_dev + l) * halves + h]

    def pack(b):
        if 0 < b < last:
            return mid[base + b - 1]
        ref = above if b < 0 else top if b == 0 else bottom if b == last else below
        return ref[edge]

    outer = outer_rows(rows)
    value = smooth_rows(outer, cell, pack, level_dev, cols, *scratch, (wm, ws))
    for i in outer:
        for l in range(level_dev):
            for h in range(halves):
                o_ref[h, pl.ds(l * SUB * rows + i, SUB, stride=rows), :] = value(i, l, h)


def outer_smooth(above, top, mid, bottom, below, weights, level_dev, rows, cols):
    return pl.pallas_call(
        functools.partial(outer_kernel, level_dev, rows, cols),
        out_shape=jax.ShapeDtypeStruct((cols // LANES, level_dev * SUB * rows, LANES), F32),
        in_specs=[VMEM] * 7,
        out_specs=VMEM,
        scratch_shapes=scratch_of(outer_rows(rows), level_dev, cols),
        compiler_params=LIMIT,
        name="outer",
    )(above, top, mid, bottom, below, *weights)


def scale_kernel(cells, factor, groups, md, first_ref, *refs):
    s_refs = refs[:groups]
    inside, outside, part, mean_hbm, out_hbm, m_ref, mean_ref, out, sem = refs[groups:]
    level_dev, rows, cols = mean_ref.shape
    halves = cols // LANES
    first = first_ref[0]
    spread = jnp.sum(part[...], keepdims=True) / cells
    inverse = (1.0 / ((spread + 1e-06) * factor))[None]
    shape = (SUB, rows, LANES)
    row = lax.broadcasted_iota(jnp.int32, shape, 1)
    inner = (row >= REACH) & (row < rows - REACH)
    copies = []
    for l in range(level_dev):
        for h in range(halves):
            at = slice(l * SUB * rows, (l + 1) * SUB * rows)
            v = jnp.where(inner, inside[h, at, :].reshape(shape), outside[h, at, :].reshape(shape))
            out[l * SUB : (l + 1) * SUB, :, h * LANES : (h + 1) * LANES] = v * inverse
        pairs = pl.ds(l * SUB, SUB)
        copies.append(pltpu.make_async_copy(out.at[pairs], out_hbm.at[pairs], sem.at[l]))
        copies[-1].start()
    scale = 1.0 / (FACTOR * FACTOR * groups * md)
    for i in range(rows):
        for h in range(halves):
            total = functools.reduce(jnp.add, [s[i * halves + h] for s in s_refs])
            m_ref[h, pl.ds(i, SUB, stride=rows), :] = total * scale
    for l in range(level_dev):
        start = pl.multiple_of((first + l) * rows, SUB)
        for h in range(halves):
            mean_ref[l, :, h * LANES : (h + 1) * LANES] = m_ref[h, pl.ds(start, rows), :]
    copies.append(pltpu.make_async_copy(mean_ref, mean_hbm, sem.at[level_dev]))
    copies[-1].start()
    for copy in copies:
        copy.wait()


def scaled(first, sums, inside, outside, part, cells, factor, md, level_dev, rows, cols):
    groups = len(sums)
    mean_shape, out_shape = (level_dev, rows, cols), (level_dev * SUB, rows, cols)
    return pl.pallas_call(
        functools.partial(scale_kernel, cells, float(factor), groups, md),
        out_shape=(jax.ShapeDtypeStruct(mean_shape, F32), jax.ShapeDtypeStruct(out_shape, F32)),
        in_specs=[SMEM] + [VMEM] * (groups + 3),
        out_specs=(HBM, HBM),
        scratch_shapes=[
            pltpu.VMEM((cols // LANES, SUB * rows, LANES), F32),
            pltpu.VMEM(mean_shape, F32),
            pltpu.VMEM(out_shape, F32),
            pltpu.SemaphoreType.DMA((level_dev + 1,)),
        ],
        compiler_params=LIMIT,
        name="scale",
    )(first, *sums, inside, outside, part)


def shift(x, axis, by):
    devices = lax.axis_size(axis)
    return lax.ppermute(x, axis, [(i, i + by) for i in range(devices) if 0 <= i + by < devices])


def neighbours(initial, last, axis):
    devices = lax.axis_size(axis)
    if axis not in PAIRED:
        before = shift(last, axis, 1)
        after = shift(initial, axis, -1)
        return before, after
    odd = lax.axis_index(axis) % 2 == 1
    received = []
    for parity in range(2):
        pairs = [(i, i + 1) for i in range(parity, devices - 1, 2)]
        send = jnp.where(odd, initial, last) if parity == 0 else jnp.where(odd, last, initial)
        perm = pairs + [(b, a) for a, b in pairs]
        received.append(lax.ppermute(send, axis, perm))
    return jnp.where(odd, received[0], received[1]), jnp.where(odd, received[1], received[0])


def rotate(x, axis, by):
    devices = lax.axis_size(axis)
    return lax.ppermute(x, axis, [(i, (i + by) % devices) for i in range(devices)])


def everyone(x, axis):
    return [x] + [rotate(x, axis, by) for by in range(1, lax.axis_size(axis))]


def across(x, order):
    for axis in sorted({axis for axis, _ in order}):
        devices = lax.axis_size(axis)
        if devices & (devices - 1):
            x = functools.reduce(jnp.add, everyone(x, axis))
    steps = [(axis, bit) for bit in range(32) for axis in ("sx", "sy") if 1 << bit < lax.axis_size(axis)]
    for axis, bit in sorted(steps, key=lambda step: order.index(step) if step in order else len(order)):
        devices = lax.axis_size(axis)
        if devices & (devices - 1) == 0:
            x = x + lax.ppermute(x, axis, [(i, i ^ (1 << bit)) for i in range(devices)])
    return x


def local(child):
    md, levels, child_rows, child_cols = child.shape
    rows, cols = child_rows // FACTOR, child_cols // FACTOR
    halves = cols // LANES
    groups = lax.axis_size("mem")
    level_dev = levels // groups
    first = (lax.axis_index("mem") * level_dev).astype(jnp.int32).reshape(1)
    main, side = window_matrices(cols)
    factor = rounded_window()
    weights = ((main * factor).astype(BF16), (side * factor).astype(BF16))
    s, h_edge, h_mid, right, left = pool(child, md * groups)
    sums = everyone(s, "mem")
    edges = everyone(h_edge, "mem")
    from_left, from_right = neighbours(left, right, "sy")
    lane = lax.broadcasted_iota(jnp.int32, from_left.shape, 2)
    pack = jnp.where(lane % SIDES < REACH, from_left, from_right)
    packs = everyone(pack, "mem")
    mids = everyone(h_mid, "mem")
    part = partial_variance(sums, md)
    part = across(part, STEPS)
    top, bottom = edge_cov(first, sums, edges, packs, md, level_dev, rows, halves)
    above, below = neighbours(top, bottom, "sx")
    mid, inside = inner_smooth(first, sums, mids, packs, top, bottom, weights, md, level_dev, rows, cols)
    cells = levels * rows * lax.axis_size("sx") * cols * lax.axis_size("sy")
    outside = outer_smooth(above, top, mid, bottom, below, weights, level_dev, rows, cols)
    parent_mean, local_cov = scaled(
        first, sums, inside, outside, part, cells, factor, md, level_dev, rows, cols
    )
    return (parent_mean, local_cov)


def solution(mesh):
    in_specs = (P("mem", None, "sx", "sy"),)
    out_specs = (P("mem", "sx", "sy"), P("mem", "sx", "sy"))
    return jax.shard_map(local, mesh=mesh, in_specs=in_specs, out_specs=out_specs, check_vma=False)
```

```python
import functools
import math

import jax
import jax.numpy as jnp
import numpy as np
from jax import lax
from jax.experimental import pallas as pl
from jax.experimental.pallas import tpu as pltpu
from jax.sharding import PartitionSpec as P


PAIRED = ("sx", "sy")
STEPS = (('sx', 0), ('sx', 1), ('sy', 0), ('sy', 1))

REACH = 4
FACTOR = 3
SUB = 8
LANES = 128
SIDES = 2 * REACH
VMEM = pl.BlockSpec(memory_space=pltpu.VMEM)
SMEM = pl.BlockSpec(memory_space=pltpu.SMEM)
HBM = pl.BlockSpec(memory_space=pltpu.HBM)
LIMIT = pltpu.CompilerParams(vmem_limit_bytes=16 << 20)
F32 = jnp.float32
BF16 = jnp.bfloat16


def gaspari_table(reach):
    offsets = np.arange(-reach, reach + 1) * 1.0
    dist = np.sqrt(offsets[:, None] ** 2 + offsets[None, :] ** 2) / 2.5
    near = -0.25 * dist**5 + 0.5 * dist**4 + 0.625 * dist**3 - 5.0 / 3.0 * dist**2 + 1.0
    safe = np.maximum(dist, 0.001)
    far = (
        dist**5 / 12.0
        - 0.5 * dist**4
        + 0.625 * dist**3
        + 5.0 / 3.0 * dist**2
        - 5.0 * dist
        + 4.0
        - 2.0 / (3.0 * safe)
    )
    table = np.where(dist <= 1.0, near, np.where(dist < 2.0, far, 0.0))
    return table / table.sum()


def window_matrices(cols):
    table = gaspari_table(REACH)

    def weight(di, dj):
        inside = (abs(di) <= REACH) & (abs(dj) <= REACH)
        return np.where(inside, table[np.clip(di, -REACH, REACH) + REACH, np.clip(dj, -REACH, REACH) + REACH], 0.0)

    src, dst = np.arange(cols)[:, None], np.arange(cols)[None, :]
    main = np.concatenate([weight(np.full((cols, cols), d), src - dst) for d in range(REACH + 1)])
    columns = np.concatenate([np.arange(-REACH, 0), np.arange(cols, cols + REACH)])
    side = np.zeros((LANES, REACH * cols))
    for block in range(3):
        for row in range(REACH):
            for col in range(SIDES):
                lane = (block * REACH + row) * SIDES + col
                for to in range(REACH):
                    di = block * REACH + row - to - REACH
                    side[lane, to * cols : (to + 1) * cols] = weight(
                        np.full((cols,), di), columns[col] - np.arange(cols)
                    )
    return main, side


def rounded_window():
    table = gaspari_table(REACH)
    best = None
    for factor in np.linspace(1.0, 2.0, 4097)[:-1]:
        error = (table * factor).astype(BF16).astype(np.float64) / factor - table
        worst = max(np.sqrt((error**2).sum() / (table**2).sum()), abs(error.sum()))
        if best is None or worst < best[0]:
            best = (worst, factor)
    return best[1]


def lanes(start, width):
    lane = lax.broadcasted_iota(jnp.int32, (SUB, LANES), 1)
    return (lane >= start) & (lane < start + width)


def placed(i, rows):
    if i < REACH:
        return True, i
    if i < rows - REACH:
        return False, i - REACH
    return True, i - (rows - SIDES)


def pool_kernel(members, child, s_ref, edge_ref, mid_ref, right_ref, left_ref, buf, pmat, even_ref, odd_ref, sem):
    md, levels, child_rows, child_cols = child.shape
    rows, cols = child_rows // FACTOR, child_cols // FACTOR
    halves = cols // LANES
    wide = FACTOR * LANES
    copies = [pltpu.make_async_copy(child.at[m], buf.at[m], sem.at[m]) for m in range(md)]
    for copy in copies:
        copy.start()
    gap = lax.broadcasted_iota(jnp.int32, (wide, LANES), 0) - FACTOR * lax.broadcasted_iota(
        jnp.int32, (wide, LANES), 1
    )
    pmat[...] = jnp.where((gap >= 0) & (gap < FACTOR), 1.0, 0.0).astype(BF16)
    place = lax.broadcasted_iota(jnp.int32, (SUB, LANES), 1) >> (REACH.bit_length() - 1)
    norm = 1.0 / (FACTOR * FACTOR * math.sqrt(members - 1))
    partial = jnp.zeros((SUB, LANES), F32)

    def packed(g, c, sides):
        for ref, values, spare in ((right_ref, sides[0], LANES - REACH), (left_ref, sides[1], -REACH)):
            pack = ref[g]
            for ri, v in enumerate(values):
                base = (c * REACH + ri) * SIDES
                at = base // REACH + (spare < 0)
                pack = jnp.where(place == at, pltpu.roll(v, (base - spare) % LANES, 1), pack)
            ref[g] = pack

    for g in range(rows // REACH):
        right_ref[g] = jnp.zeros((SUB, LANES), F32)
        left_ref[g] = jnp.zeros((SUB, LANES), F32)
    blocks = rows // REACH

    sums_of = (even_ref, odd_ref)
    height = levels * child_rows
    chunk = levels // 2
    products = halves * (levels // chunk)

    def product(m, n):
        h, start = n % halves, n // halves * chunk
        x = buf[m, start : start + chunk, :, h * wide : (h + 1) * wide].reshape(chunk * child_rows, wide)
        at = h * height + start * child_rows
        sums_of[m % 2][at : at + chunk * child_rows, :] = jnp.dot(x, pmat[...], preferred_element_type=F32)

    def fields(m, g, partial):
        contrasts, totals = ([], []), ([], [])
        for ri in range(REACH):
            i = g * REACH + ri
            outer, at = placed(i, rows)
            h_ref = edge_ref if outer else mid_ref
            for h in range(halves):
                slot = i * halves + h
                parts = [
                    sums_of[m % 2][pl.ds(h * height + FACTOR * i + a, levels, stride=child_rows), :]
                    for a in range(FACTOR)
                ]
                p = parts[0] + parts[1] + parts[2]
                if m == 0:
                    s_ref[slot] = p
                    continue
                total = s_ref[slot]
                contrast = (total - m * p) * (norm / math.sqrt(m * (m + 1)))
                total = total + p
                h_ref[(at * (md - 1) + m - 1) * halves + h] = contrast
                s_ref[slot] = total
                partial = partial + contrast * contrast
                if h == halves - 1:
                    contrasts[0].append(contrast)
                    totals[0].append(total)
                if h == 0:
                    contrasts[1].append(contrast)
                    totals[1].append(total)
        if m > 0:
            packed(g, m, contrasts)
        if m == md - 1:
            packed(g, 0, totals)
        return partial

    for m in range(md + 1):
        if m < md:
            copies[m].wait()
        for n in range(max(products, blocks)):
            if m < md and n < products:
                product(m, n)
            if m > 0 and n < blocks:
                partial = fields(m - 1, n, partial)
    s_ref[rows * halves] = partial


def pool(child, members):
    md, levels, child_rows, child_cols = child.shape
    rows, cols = child_rows // FACTOR, child_cols // FACTOR
    halves = cols // LANES
    tile = (SUB, LANES)
    return pl.pallas_call(
        functools.partial(pool_kernel, members),
        out_shape=(
            jax.ShapeDtypeStruct((rows * halves + 1,) + tile, F32),
            jax.ShapeDtypeStruct((SIDES * (md - 1) * halves,) + tile, F32),
            jax.ShapeDtypeStruct(((rows - SIDES) * (md - 1) * halves,) + tile, F32),
            jax.ShapeDtypeStruct((rows // REACH,) + tile, F32),
            jax.ShapeDtypeStruct((rows // REACH,) + tile, F32),
        ),
        in_specs=[HBM],
        out_specs=(VMEM,) * 5,
        scratch_shapes=[
            pltpu.VMEM(child.shape, BF16),
            pltpu.VMEM((FACTOR * LANES, LANES), BF16),
            pltpu.VMEM((halves * levels * child_rows, LANES), F32),
            pltpu.VMEM((halves * levels * child_rows, LANES), F32),
            pltpu.SemaphoreType.DMA((md,)),
        ],
        compiler_params=LIMIT,
        name="pool",
    )(pltpu.with_memory_space_constraint(child, pltpu.HBM))


def group_contrasts(sums, md, members):
    norm = 1.0 / (FACTOR * FACTOR * math.sqrt((members - 1) * md))
    total, out = sums[0], []
    for g in range(1, len(sums)):
        out.append((total - g * sums[g]) * (norm / math.sqrt(g * (g + 1))))
        total = total + sums[g]
    return out, total


def partial_kernel(groups, md, *refs):
    s_refs, partial_ref = refs[:groups], refs[groups]
    slots = s_refs[0].shape[0] - 1
    partial = functools.reduce(jnp.add, [s[slots] for s in s_refs])
    for slot in range(slots):
        contrasts, _ = group_contrasts([s[slot] for s in s_refs], md, groups * md)
        for v in contrasts:
            partial = partial + v * v
    partial_ref[...] = partial


def partial_variance(sums, md):
    return pl.pallas_call(
        functools.partial(partial_kernel, len(sums), md),
        out_shape=jax.ShapeDtypeStruct((SUB, LANES), F32),
        in_specs=[VMEM] * len(sums),
        out_specs=VMEM,
        compiler_params=LIMIT,
        name="partial",
    )(*sums)


def spread_row(ref, slot, row):
    return jnp.broadcast_to(ref[slot, pl.ds(row, 1), :], (SUB, LANES))


def cov_rows(chosen, first, level_dev, rows, halves, md, s_refs, h_refs, d_ref, store):
    groups = len(s_refs)
    for n, i in enumerate(chosen):
        _, at = placed(i, rows)
        for h in range(halves):
            contrasts, _ = group_contrasts([s[i * halves + h] for s in s_refs], md, groups * md)
            where = []
            for g, v in enumerate(contrasts):
                slot = (n * halves + h) * (groups - 1) + g
                d_ref[slot] = v
                where.append((d_ref, slot))
            for ref in h_refs:
                where += [(ref, (at * (md - 1) + c) * halves + h) for c in range(md - 1)]
            values = [ref[slot] for ref, slot in where]
            for l in range(level_dev):
                acc = None
                for (ref, slot), v in zip(where, values):
                    term = spread_row(ref, slot, first + l) * v
                    acc = term if acc is None else acc + term
                store(i, l, h, acc)


def cov_packs(chosen, first, level_dev, md, e_refs, x_ref, store):
    groups = len(e_refs)
    width = LANES // md
    for n, b in enumerate(chosen):
        packs = [e[b] for e in e_refs]
        contrasts, _ = group_contrasts(packs, md, groups * md)
        for g in range(groups):
            inner = jnp.zeros((SUB, LANES), F32) if g == 0 else contrasts[g - 1]
            x_ref[n * groups + g] = jnp.where(lanes(0, width), inner, packs[g])
        pack = jnp.zeros((SUB, LANES), F32)
        for l in range(level_dev):
            acc = None
            for g in range(groups):
                term = spread_row(x_ref, n * groups + g, first + l) * x_ref[n * groups + g]
                acc = term if acc is None else acc + term
            total = acc
            for c in range(1, md):
                total = total + pltpu.roll(acc, c * width, 1)
            pack = jnp.where(lanes(l * width, width), total, pack)
        store(b, pack)


def smooth_rows(chosen, cell, pack, level_dev, cols, x_ref, e_ref, weights):
    halves = cols // LANES

    def put(ref, at, columns, v):
        hi = v.astype(BF16)
        ref[at : at + 2 * SUB, columns] = hi
        at += ref.shape[0] // 2
        ref[at : at + 2 * SUB, columns] = (v - hi.astype(F32)).astype(BF16)

    order = [(i, l) for i in chosen for l in range(level_dev)]
    for q in range(0, len(order), 2):
        for h in range(halves):
            for d in range(REACH + 1):
                pair = []
                for i, l in order[q : q + 2]:
                    v = cell(i - d, l, h)
                    if d:
                        v = v + cell(i + d, l, h)
                    pair.append(v)
                columns = slice(d * cols + h * LANES, d * cols + (h + 1) * LANES)
                put(x_ref, q * SUB, columns, jnp.concatenate(pair, axis=0))
    width = REACH * SIDES
    blocks = sorted({i // REACH for i in chosen})
    order = [(b, l) for b in blocks for l in range(level_dev)]
    for q in range(0, len(order), 2):
        pair = []
        for b, l in order[q : q + 2]:
            v = jnp.zeros((SUB, LANES), F32)
            for g in range(3):
                moved = pack(b + g - 1)
                if g != l:
                    moved = pltpu.roll(moved, ((g - l) * width) % LANES, 1)
                v = jnp.where(lanes(g * width, width), moved, v)
            pair.append(v)
        put(e_ref, q * SUB, slice(0, LANES), jnp.concatenate(pair, axis=0))

    def product(ref, w):
        both = jnp.dot(ref[...], w[...], preferred_element_type=F32)
        return both[: ref.shape[0] // 2] + both[ref.shape[0] // 2 :]

    y = product(x_ref, weights[0])
    z = product(e_ref, weights[1])

    def value(i, l, h):
        n = chosen.index(i)
        at = (blocks.index(i // REACH) * level_dev + l) * SUB
        side = (i % REACH) * cols + h * LANES
        return (
            y[(n * level_dev + l) * SUB : (n * level_dev + l + 1) * SUB, h * LANES : (h + 1) * LANES]
            + z[at : at + SUB, side : side + LANES]
        )

    return value


def scratch_of(chosen, level_dev, cols):
    rows = len(chosen) * level_dev * SUB
    sides = rows // REACH
    return [
        pltpu.VMEM((2 * rows, (REACH + 1) * cols), BF16),
        pltpu.VMEM((2 * sides, LANES), BF16),
    ]


def outer_rows(rows):
    return list(range(REACH)) + list(range(rows - REACH, rows))


def inner_rows(rows):
    return list(range(REACH, rows - REACH))


def edge_kernel(groups, md, level_dev, rows, halves, first_ref, *refs):
    s_refs, h_refs, e_refs = refs[:groups], refs[groups : 2 * groups], refs[2 * groups : 3 * groups]
    top_ref, bottom_ref, d_ref, x_ref = refs[3 * groups :]
    first = first_ref[0]
    edge = REACH * level_dev * halves

    def store(i, l, h, v):
        ref = top_ref if i < REACH else bottom_ref
        ref[(i % REACH * level_dev + l) * halves + h] = v

    def store_pack(b, v):
        ref = top_ref if b == 0 else bottom_ref
        ref[edge] = v

    cov_packs([0, rows // REACH - 1], first, level_dev, md, e_refs, x_ref, store_pack)
    cov_rows(outer_rows(rows), first, level_dev, rows, halves, md, s_refs, h_refs, d_ref, store)


def edge_cov(first, sums, contrasts, packs, md, level_dev, rows, halves):
    groups = len(sums)
    shape = jax.ShapeDtypeStruct((REACH * level_dev * halves + 1, SUB, LANES), F32)
    return pl.pallas_call(
        functools.partial(edge_kernel, groups, md, level_dev, rows, halves),
        out_shape=(shape, shape),
        in_specs=[SMEM] + [VMEM] * (3 * groups),
        out_specs=(VMEM, VMEM),
        scratch_shapes=[
            pltpu.VMEM(((groups - 1) * SIDES * halves, SUB, LANES), F32),
            pltpu.VMEM((groups * 2, SUB, LANES), F32),
        ],
        compiler_params=pltpu.CompilerParams(vmem_limit_bytes=16 << 20),
        name="edge",
    )(first, *sums, *contrasts, *packs)


def inner_kernel(groups, md, level_dev, rows, cols, first_ref, *refs):
    s_refs, h_refs, e_refs = refs[:groups], refs[groups : 2 * groups], refs[2 * groups : 3 * groups]
    top, bottom, wm, ws, mid_ref, o_ref, d_ref, x_ref = refs[3 * groups : 3 * groups + 8]
    scratch = refs[3 * groups + 8 :]
    halves = cols // LANES
    first = first_ref[0]
    edge = REACH * level_dev * halves
    base = (rows - SIDES) * level_dev * halves

    def store(i, l, h, v):
        mid_ref[((i - REACH) * level_dev + l) * halves + h] = v

    def store_pack(b, v):
        mid_ref[base + b - 1] = v

    inner = inner_rows(rows)
    last = rows // REACH - 1
    cov_packs(list(range(1, last)), first, level_dev, md, e_refs, x_ref, store_pack)
    cov_rows(inner, first, level_dev, rows, halves, md, s_refs, h_refs, d_ref, store)

    def cell(i, l, h):
        if i < REACH:
            return top[(i * level_dev + l) * halves + h]
        if i >= rows - REACH:
            return bottom[((i - rows + REACH) * level_dev + l) * halves + h]
        return mid_ref[((i - REACH) * level_dev + l) * halves + h]

    def pack(b):
        if b == 0:
            return top[edge]
        return bottom[edge] if b == last else mid_ref[base + b - 1]

    value = smooth_rows(inner, cell, pack, level_dev, cols, *scratch, (wm, ws))
    for i in inner:
        for l in range(level_dev):
            for h in range(halves):
                o_ref[h, pl.ds(l * SUB * rows + i, SUB, stride=rows), :] = value(i, l, h)


def inner_smooth(first, sums, contrasts, packs, top, bottom, weights, md, level_dev, rows, cols):
    groups = len(sums)
    halves = cols // LANES
    slots = (rows - SIDES) * level_dev * halves + rows // REACH - 2
    inner = inner_rows(rows)
    return pl.pallas_call(
        functools.partial(inner_kernel, groups, md, level_dev, rows, cols),
        out_shape=(
            jax.ShapeDtypeStruct((slots, SUB, LANES), F32),
            jax.ShapeDtypeStruct((halves, level_dev * SUB * rows, LANES), F32),
        ),
        in_specs=[SMEM] + [VMEM] * (3 * groups + 4),
        out_specs=(VMEM, VMEM),
        scratch_shapes=[
            pltpu.VMEM(((groups - 1) * len(inner) * halves, SUB, LANES), F32),
            pltpu.VMEM((groups * (rows // REACH - 2), SUB, LANES), F32),
        ]
        + scratch_of(inner, level_dev, cols),
        compiler_params=LIMIT,
        name="inner",
    )(first, *sums, *contrasts, *packs, top, bottom, *weights)


def outer_kernel(level_dev, rows, cols, above, top, mid, bottom, below, wm, ws, o_ref, *scratch):
    halves = cols // LANES
    edge = REACH * level_dev * halves
    base = (rows - SIDES) * level_dev * halves
    last = rows // REACH - 1

    def cell(i, l, h):
        if i < 0:
            ref, row = above, i + REACH
        elif i < REACH:
            ref, row = top, i
        elif i < rows - REACH:
            ref, row = mid, i - REACH
        elif i < rows:
            ref, row = bottom, i - rows + REACH
        else:
            ref, row = below, i - rows
        return ref[(row * level_dev + l) * halves + h]

    def pack(b):
        if 0 < b < last:
            return mid[base + b - 1]
        ref = above if b < 0 else top if b == 0 else bottom if b == last else below
        return ref[edge]

    outer = outer_rows(rows)
    value = smooth_rows(outer, cell, pack, level_dev, cols, *scratch, (wm, ws))
    for i in outer:
        for l in range(level_dev):
            for h in range(halves):
                o_ref[h, pl.ds(l * SUB * rows + i, SUB, stride=rows), :] = value(i, l, h)


def outer_smooth(above, top, mid, bottom, below, weights, level_dev, rows, cols):
    return pl.pallas_call(
        functools.partial(outer_kernel, level_dev, rows, cols),
        out_shape=jax.ShapeDtypeStruct((cols // LANES, level_dev * SUB * rows, LANES), F32),
        in_specs=[VMEM] * 7,
        out_specs=VMEM,
        scratch_shapes=scratch_of(outer_rows(rows), level_dev, cols),
        compiler_params=LIMIT,
        name="outer",
    )(above, top, mid, bottom, below, *weights)


def scale_kernel(cells, factor, groups, md, first_ref, *refs):
    s_refs = refs[:groups]
    inside, outside, part, mean_hbm, out_hbm, m_ref, mean_ref, out, sem = refs[groups:]
    level_dev, rows, cols = mean_ref.shape
    halves = cols // LANES
    first = first_ref[0]
    spread = jnp.sum(part[...], keepdims=True) / cells
    inverse = (1.0 / ((spread + 1e-06) * factor))[None]
    shape = (SUB, rows, LANES)
    row = lax.broadcasted_iota(jnp.int32, shape, 1)
    inner = (row >= REACH) & (row < rows - REACH)
    copies = []
    for l in range(level_dev):
        for h in range(halves):
            at = slice(l * SUB * rows, (l + 1) * SUB * rows)
            v = jnp.where(inner, inside[h, at, :].reshape(shape), outside[h, at, :].reshape(shape))
            out[l * SUB : (l + 1) * SUB, :, h * LANES : (h + 1) * LANES] = v * inverse
        pairs = pl.ds(l * SUB, SUB)
        copies.append(pltpu.make_async_copy(out.at[pairs], out_hbm.at[pairs], sem.at[l]))
        copies[-1].start()
    scale = 1.0 / (FACTOR * FACTOR * groups * md)
    for i in range(rows):
        for h in range(halves):
            total = functools.reduce(jnp.add, [s[i * halves + h] for s in s_refs])
            m_ref[h, pl.ds(i, SUB, stride=rows), :] = total * scale
    for l in range(level_dev):
        start = pl.multiple_of((first + l) * rows, SUB)
        for h in range(halves):
            mean_ref[l, :, h * LANES : (h + 1) * LANES] = m_ref[h, pl.ds(start, rows), :]
    copies.append(pltpu.make_async_copy(mean_ref, mean_hbm, sem.at[level_dev]))
    copies[-1].start()
    for copy in copies:
        copy.wait()


def scaled(first, sums, inside, outside, part, cells, factor, md, level_dev, rows, cols):
    groups = len(sums)
    mean_shape, out_shape = (level_dev, rows, cols), (level_dev * SUB, rows, cols)
    return pl.pallas_call(
        functools.partial(scale_kernel, cells, float(factor), groups, md),
        out_shape=(jax.ShapeDtypeStruct(mean_shape, F32), jax.ShapeDtypeStruct(out_shape, F32)),
        in_specs=[SMEM] + [VMEM] * (groups + 3),
        out_specs=(HBM, HBM),
        scratch_shapes=[
            pltpu.VMEM((cols // LANES, SUB * rows, LANES), F32),
            pltpu.VMEM(mean_shape, F32),
            pltpu.VMEM(out_shape, F32),
            pltpu.SemaphoreType.DMA((level_dev + 1,)),
        ],
        compiler_params=LIMIT,
        name="scale",
    )(first, *sums, inside, outside, part)


def shift(x, axis, by):
    devices = lax.axis_size(axis)
    return lax.ppermute(x, axis, [(i, i + by) for i in range(devices) if 0 <= i + by < devices])


def neighbours(initial, last, axis):
    devices = lax.axis_size(axis)
    if axis not in PAIRED:
        before = shift(last, axis, 1)
        after = shift(initial, axis, -1)
        return before, after
    odd = lax.axis_index(axis) % 2 == 1
    received = []
    for parity in range(2):
        pairs = [(i, i + 1) for i in range(parity, devices - 1, 2)]
        send = jnp.where(odd, initial, last) if parity == 0 else jnp.where(odd, last, initial)
        perm = pairs + [(b, a) for a, b in pairs]
        received.append(lax.ppermute(send, axis, perm))
    return jnp.where(odd, received[0], received[1]), jnp.where(odd, received[1], received[0])


def rotate(x, axis, by):
    devices = lax.axis_size(axis)
    return lax.ppermute(x, axis, [(i, (i + by) % devices) for i in range(devices)])


def everyone(x, axis):
    return [x] + [rotate(x, axis, by) for by in range(1, lax.axis_size(axis))]


def across(x, order):
    for axis in sorted({axis for axis, _ in order}):
        devices = lax.axis_size(axis)
        if devices & (devices - 1):
            x = functools.reduce(jnp.add, everyone(x, axis))
    steps = [(axis, bit) for bit in range(32) for axis in ("sx", "sy") if 1 << bit < lax.axis_size(axis)]
    for axis, bit in sorted(steps, key=lambda step: order.index(step) if step in order else len(order)):
        devices = lax.axis_size(axis)
        if devices & (devices - 1) == 0:
            rows, cols = lax.axis_size("sx"), lax.axis_size("sy")
            up, along = (1 << bit, 0) if axis == "sx" else (0, 1 << bit)
            if cols % 2 == 0:
                along |= 1
            pairs = [(r * cols + c, (r ^ up) * cols + (c ^ along)) for r in range(rows) for c in range(cols)]
            x = x + lax.ppermute(x, ("sx", "sy"), pairs)
    return x


def local(child):
    md, levels, child_rows, child_cols = child.shape
    rows, cols = child_rows // FACTOR, child_cols // FACTOR
    halves = cols // LANES
    groups = lax.axis_size("mem")
    level_dev = levels // groups
    first = (lax.axis_index("mem") * level_dev).astype(jnp.int32).reshape(1)
    main, side = window_matrices(cols)
    factor = rounded_window()
    weights = ((main * factor).astype(BF16), (side * factor).astype(BF16))
    s, h_edge, h_mid, right, left = pool(child, md * groups)
    sums = everyone(s, "mem")
    edges = everyone(h_edge, "mem")
    from_left, from_right = neighbours(left, right, "sy")
    lane = lax.broadcasted_iota(jnp.int32, from_left.shape, 2)
    pack = jnp.where(lane % SIDES < REACH, from_left, from_right)
    packs = everyone(pack, "mem")
    mids = everyone(h_mid, "mem")
    part = partial_variance(sums, md)
    part = across(part, STEPS)
    top, bottom = edge_cov(first, sums, edges, packs, md, level_dev, rows, halves)
    above, below = neighbours(top, bottom, "sx")
    mid, inside = inner_smooth(first, sums, mids, packs, top, bottom, weights, md, level_dev, rows, cols)
    cells = levels * rows * lax.axis_size("sx") * cols * lax.axis_size("sy")
    outside = outer_smooth(above, top, mid, bottom, below, weights, level_dev, rows, cols)
    parent_mean, local_cov = scaled(
        first, sums, inside, outside, part, cells, factor, md, level_dev, rows, cols
    )
    return (parent_mean, local_cov)


def solution(mesh):
    in_specs = (P("mem", None, "sx", "sy"),)
    out_specs = (P("mem", "sx", "sy"), P("mem", "sx", "sy"))
    return jax.shard_map(local, mesh=mesh, in_specs=in_specs, out_specs=out_specs, check_vma=False)
```
